512 devices in a mesh: blk: 64 (over y, x, core), pts: 8 (over z).
Axes of the slice: x: 4, y: 8, z: 8, core: 2. Of those that a mesh axis runs over, the one named last changes fastest.
Arguments:
- snapshots: float32 [16384, 5, 1024], P('blk', None, 'pts'), may hold values from -150 to 150
- weights: float32 [5, 1024], P(None, 'pts'), may hold values from 0.3 to 3
- offsets: int32 [64], replicated, may hold values from 0 to 255, as said below
- freqs: int32 [64], replicated, may hold values from 1 to 127, as said below
Outputs:
- modes: float32 [64, 64, 2, 5, 1024], P('blk', None, None, None, 'pts')
- spectrum: float32 [64, 64], P('blk')
The draws below stay inside these ranges and needn't reach their ends.
Inputs may be any that keep to these rules, and one draw needn't show every extreme that they name: Block b covers snapshots b * 256 + offsets[b] onward, 256 of them; the last block's offset is 0 and some other block's is 255. `freqs`: distinct and increasing; 1 and 127 are among them.
All inputs are finite; a program needn't handle non-finite values.
Results may differ from the reference program's by a relative error of at most 0.008.
Values sent between devices are 32-bit elements; how exact they have to be, the bound alone decides.
No kernel may reach another device: no remote copies, remote signals or barrier semaphores. Data moves between devices by JAX's collectives and lax.ppermute only.
A program may use at most 64 MiB of HBM per device.

```python
import math
import jax
import jax.numpy as jnp
from jax import lax

NFFT = 256
NF = 64
VARS = 5
SWEEPS = 2
NB = 64
NT = 16384
NP = 1024


def draw_snapshots(key, part):
    key_noise, key_amp, key_shape, key_scale = jax.random.split(key, 4)
    width = VARS * NP
    times = jnp.arange(NT, dtype=jnp.float32) / NT
    envelope = 1.0 + 2.0 * times
    amplitude = jax.random.normal(key_amp, (NT, 4), jnp.float32)
    pattern = jax.random.normal(key_shape, (4, width), jnp.float32)
    point_scale = jnp.exp(jax.random.uniform(key_scale, (1, width), jnp.float32, 0.0, 2.3))
    white = jnp.clip(jax.random.normal(key_noise, (NT + 1, width), jnp.float32), -4.0, 4.0)
    level = 0.7
    colored = level * white[1:] + (white[1:] - white[:-1])
    field = colored * point_scale
    field = field + amplitude[:, 0:1] * pattern[0:1]
    field = field + amplitude[:, 1:2] * pattern[1:2]
    field = field + amplitude[:, 2:3] * pattern[2:3]
    field = field + amplitude[:, 3:4] * pattern[3:4]
    field = jnp.clip(envelope[:, None] * field, -150.0, 150.0)
    return field.reshape(NT, VARS, NP)


def draw_offsets(key, part):
    key_base, key_pick = jax.random.split(key, 2)
    drawn = jax.random.randint(key_base, (NB,), 0, NFFT, dtype=jnp.int32)
    chosen = jax.random.randint(key_pick, (), 0, NB - 1, dtype=jnp.int32)
    position = jnp.arange(NB, dtype=jnp.int32)
    drawn = jnp.where(position == chosen, NFFT - 1, drawn)
    return jnp.where(position == NB - 1, 0, drawn).astype(jnp.int32)


def draw_freqs(key, part):
    interior = 2 + jax.random.permutation(key, NFFT // 2 - 3)[:NF - 2].astype(jnp.int32)
    picked = jnp.concatenate([jnp.array([1, NFFT // 2 - 1], dtype=jnp.int32), interior])
    return jnp.sort(picked).astype(jnp.int32)


def steps_of(stream_key, dims, cuts, low, top_value):
    def one(dim, shards_of):
        steps = jax.random.uniform(jax.random.fold_in(jax.random.fold_in(stream_key, 6), dim), (shards_of,), jnp.float32, low / len(cuts), top_value / len(cuts))
        return jnp.repeat(jnp.exp(steps), dims[dim] // shards_of).reshape((-1,) + (1,) * (len(dims) - dim - 1))

    factor_of = one(*cuts[0])
    for cut in cuts[1:]:
        factor_of = factor_of * one(*cut)
    return factor_of


def setup_inputs(seed: int = 0) -> dict:
    streams_of = jax.random.split(jax.random.key(seed), 5)
    snapshots = draw_snapshots(jax.random.fold_in(streams_of[4], 71), 0)
    weights = jnp.clip(jnp.exp(math.log(3.0) - 2.3025851 * jax.random.uniform(streams_of[1], (VARS, NP), jnp.float32) ** steps_of(streams_of[1], (VARS, NP), ((1, 8),), -0.2, 0.2)), 0.3, 3.0)
    offsets = draw_offsets(jax.random.fold_in(streams_of[4], 71), 0)
    freqs = draw_freqs(jax.random.fold_in(streams_of[4], 71), 0)
    return dict(snapshots=snapshots, weights=weights, offsets=offsets, freqs=freqs)


HIGH = lax.Precision.HIGHEST
DAMPING = 0.01

def spectral_table(freqs, lags, valid, nfft):
    phase_index = jnp.mod(freqs[:, None] * lags[None, :], nfft)
    angle = 2.0 * math.pi / nfft * phase_index.astype(jnp.float32)
    hann = 0.5 - 0.5 * jnp.cos(2.0 * math.pi / nfft * lags.astype(jnp.float32))
    factor = jnp.where(valid, hann, 0.0) / math.sqrt(nfft)
    table = jnp.stack([factor[None, :] * jnp.cos(angle), -factor[None, :] * jnp.sin(angle)], axis=1)
    return table.reshape(2 * freqs.shape[0], nfft)

def rotate_round(carry, round_index):
    real_a, imag_a, real_v, imag_v = carry
    count = real_a.shape[-1]
    index = jnp.arange(count, dtype=jnp.int32)
    mirror = jnp.mod(2 * round_index - index, count - 1).astype(jnp.int32)
    partner = jnp.where(index == count - 1, round_index, jnp.where(index == round_index, count - 1, mirror)).astype(jnp.int32)
    parity = jnp.where(index < partner, 1.0, -1.0).astype(jnp.float32)
    diagonal = jnp.diagonal(real_a, axis1=-2, axis2=-1)
    diag_pair = jnp.take(diagonal, partner, axis=-1)
    columns = jnp.broadcast_to(partner[:, None], real_a.shape[:-1] + (1,))
    pair_real = jnp.take_along_axis(real_a, columns, axis=-1)[..., 0]
    pair_imag = jnp.take_along_axis(imag_a, columns, axis=-1)[..., 0]
    delta = parity * (diag_pair - diagonal)
    size_sq = pair_real * pair_real + pair_imag * pair_imag
    radius = jnp.sqrt(delta * delta + 4.0 * size_sq)
    upper = radius + delta + DAMPING * (diagonal + diag_pair)
    length = jnp.sqrt(upper * upper + 4.0 * size_sq)
    cosine = upper / length
    off_real = 2.0 * parity * pair_real / length
    off_imag = 2.0 * parity * pair_imag / length
    moved_real = jnp.take(off_real, partner, axis=-1)
    moved_imag = jnp.take(off_imag, partner, axis=-1)

    def right_apply(left_real, left_imag):
        swap_real = jnp.take(left_real, partner, axis=-1)
        swap_imag = jnp.take(left_imag, partner, axis=-1)
        coef_c = cosine[..., None, :]
        coef_r = moved_real[..., None, :]
        coef_i = moved_imag[..., None, :]
        return (left_real * coef_c + swap_real * coef_r - swap_imag * coef_i, left_imag * coef_c + swap_real * coef_i + swap_imag * coef_r)

    def left_apply(right_real, right_imag):
        swap_real = jnp.take(right_real, partner, axis=-2)
        swap_imag = jnp.take(right_imag, partner, axis=-2)
        coef_c = cosine[..., :, None]
        coef_r = moved_real[..., :, None]
        coef_i = moved_imag[..., :, None]
        return (right_real * coef_c + swap_real * coef_r + swap_imag * coef_i, right_imag * coef_c + swap_imag * coef_r - swap_real * coef_i)
    half_real, half_imag = right_apply(real_a, imag_a)
    new_real, new_imag = left_apply(half_real, half_imag)
    vec_real, vec_imag = right_apply(real_v, imag_v)
    return (new_real, new_imag, vec_real, vec_imag)

def jacobi_solve(gram_real, gram_imag):
    count = gram_real.shape[-1]
    identity = jnp.broadcast_to(jnp.eye(count, dtype=gram_real.dtype), gram_real.shape)
    state = (gram_real, gram_imag, identity, jnp.zeros_like(gram_real))

    def advance(counter, carry):
        return rotate_round(carry, jnp.mod(counter, count - 1).astype(jnp.int32))
    return lax.fori_loop(0, SWEEPS * (count - 1), advance, state)

def mode_factors(real_a, real_v, imag_v, nblocks):
    eigen = jnp.diagonal(real_a, axis1=-2, axis2=-1)
    sum_real = lax.optimization_barrier(jnp.sum(real_v, axis=-2))
    sum_imag = lax.optimization_barrier(jnp.sum(imag_v, axis=-2))
    magnitude = jnp.sqrt(sum_real * sum_real + sum_imag * sum_imag)
    scaling = 1.0 / (jnp.maximum(magnitude, 1.0) * jnp.sqrt(nblocks * (eigen + 1e-06)))
    phase_real = (sum_real * scaling)[..., None, :]
    phase_imag = (-sum_imag * scaling)[..., None, :]
    coef_real = real_v * phase_real - imag_v * phase_imag
    coef_imag = real_v * phase_imag + imag_v * phase_real
    return (eigen, coef_real, coef_imag)

def reference(snapshots, weights, offsets, freqs):
    ntime, nvars, npoints = snapshots.shape
    nfreq = freqs.shape[0]
    width = nvars * npoints
    lags = jnp.arange(NFFT, dtype=jnp.int32)
    table = spectral_table(freqs, lags, lags >= 0, NFFT)

    def block_spectra(block_index):
        start = (block_index * NFFT + offsets[block_index]).astype(jnp.int32)
        segment = lax.dynamic_slice(snapshots, (start, jnp.int32(0), jnp.int32(0)), (NFFT, nvars, npoints))
        return jnp.dot(table, segment.reshape(NFFT, width), precision=HIGH).reshape(nfreq, 2, width)
    spectra = lax.map(block_spectra, jnp.arange(NB, dtype=jnp.int32))
    flat_weights = weights.reshape(1, width)
    gram_scale = 1.0 / (NB * nvars * npoints)

    def gram_of(freq_index):
        piece = lax.dynamic_index_in_dim(spectra, freq_index, 1, keepdims=False)
        part_real = piece[:, 0]
        part_imag = piece[:, 1]
        weighted_real = part_real * flat_weights
        weighted_imag = part_imag * flat_weights
        gram_real = (jnp.dot(weighted_real, part_real.T, precision=HIGH) + jnp.dot(weighted_imag, part_imag.T, precision=HIGH)) * gram_scale
        gram_imag = (jnp.dot(weighted_real, part_imag.T, precision=HIGH) - jnp.dot(weighted_imag, part_real.T, precision=HIGH)) * gram_scale
        return (gram_real, gram_imag)
    gram_real, gram_imag = lax.map(gram_of, jnp.arange(nfreq, dtype=jnp.int32))
    real_a, imag_a, real_v, imag_v = jacobi_solve(gram_real, gram_imag)
    eigen, coef_real, coef_imag = mode_factors(real_a, real_v, imag_v, NB)

    def modes_of(freq_index):
        piece = lax.dynamic_index_in_dim(spectra, freq_index, 1, keepdims=False)
        part_real = piece[:, 0]
        part_imag = piece[:, 1]
        crl = lax.dynamic_index_in_dim(coef_real, freq_index, 0, keepdims=False)
        cim = lax.dynamic_index_in_dim(coef_imag, freq_index, 0, keepdims=False)
        mode_real = jnp.dot(crl.T, part_real, precision=HIGH) - jnp.dot(cim.T, part_imag, precision=HIGH)
        mode_imag = jnp.dot(cim.T, part_real, precision=HIGH) + jnp.dot(crl.T, part_imag, precision=HIGH)
        return jnp.stack([mode_real, mode_imag], axis=1).reshape(NB, 2, nvars, npoints)
    modes = lax.map(modes_of, jnp.arange(nfreq, dtype=jnp.int32))
    total = jnp.sum(eigen)
    spectrum = nfreq * NB * eigen / total
    return (modes, spectrum)
```

```python
import functools
import math

import jax
import jax.numpy as jnp
from jax import lax
from jax.experimental import pallas as pl
from jax.experimental.pallas import tpu as pltpu
from jax.sharding import PartitionSpec as P

SWEEPS = 2
HIGH = lax.Precision.HIGHEST
DAMPING = 0.01
F32 = jnp.float32
NFFT = 256
NB = 64
LANES = 128
GROUPS = 4
UNROLL = 7
PARAMS = pltpu.CompilerParams(vmem_limit_bytes=16 << 20)


def table_kernel(block_ref, offsets_ref, freqs_ref, table_ref):
    offset = offsets_ref[block_ref[0]]
    lag = jnp.bitwise_and(lax.broadcasted_iota(jnp.int32, (1, NFFT), 1) - offset, NFFT - 1)
    unit = 2.0 * math.pi / NFFT
    hann = (0.5 - 0.5 * jnp.cos(unit * lag.astype(F32))) / math.sqrt(NFFT)
    phase = jnp.bitwise_and(freqs_ref[...] * lag, NFFT - 1)
    angle = unit * phase.astype(F32)
    table_ref[:NB, :] = hann * jnp.cos(angle)
    table_ref[NB:, :] = -hann * jnp.sin(angle)


def spectra_kernel(scale, block_ref, offsets_ref, table_ref, own_ref, next_ref, weights_ref, out_ref, energy_ref):
    offset = offsets_ref[block_ref[0]]
    mine = lax.broadcasted_iota(jnp.int32, (NFFT, LANES), 0) >= offset
    nvars = own_ref.shape[0]
    energy = jnp.zeros((8, LANES), F32)
    for v in range(nvars):
        data = jnp.where(mine, own_ref[v], next_ref[v])
        result = jnp.dot(table_ref[...], data, precision=HIGH, preferred_element_type=F32)
        for part in range(2):
            out_ref[pl.ds(2 * v + part, NB, stride=2 * nvars), :] = result[part * NB : (part + 1) * NB]
        square = jnp.sum((result * result).reshape(-1, 8, LANES), axis=0)
        energy = energy + square * (weights_ref[v : v + 1, :] * scale)
    energy_ref[...] = energy


def gram_kernel(scale, q_ref, weights_ref, gram_ref):
    nvars = weights_ref.shape[0]
    left, right_real, right_imag = [], [], []
    for v in range(nvars):
        real = q_ref[pl.ds(2 * v, NB, stride=2 * nvars), :]
        imag = q_ref[pl.ds(2 * v + 1, NB, stride=2 * nvars), :]
        weight = weights_ref[v : v + 1, :] * scale
        left += [real * weight, imag * weight]
        right_real += [real, imag]
        right_imag += [imag, -real]
    right = jnp.concatenate([jnp.concatenate(right_real, 1), jnp.concatenate(right_imag, 1)], 0)
    gram_ref[...] = lax.dot_general(
        jnp.concatenate(left, 1), right, (((1,), (1,)), ((), ())), precision=HIGH, preferred_element_type=F32
    )


def rotate(state, offset, ranks):
    top, bottom, diag_t, diag_b = state
    new_top, new_bottom, new_dt, new_db = [], [], [], []
    for v in range(GROUPS):
        zt, izt, xt, ixt = top[v]
        zb, izb, xb, ixb = bottom[v]
        real = jnp.sum(zt * xb, axis=1, keepdims=True)
        imag = jnp.sum(zt * ixb, axis=1, keepdims=True)
        at, ab = diag_t[v], diag_b[v]
        sign = jnp.where(ranks[v] > offset, 1.0, -1.0)
        delta = sign * (ab - at)
        four = 4.0 * (real * real + imag * imag)
        square = delta * delta + four
        radius = square * lax.rsqrt(jnp.maximum(square, 1e-37))
        upper = radius + delta + DAMPING * (ab + at)
        inverse = lax.rsqrt(upper * upper + four)
        cosine = upper * inverse
        twice = (sign + sign) * inverse
        off_r, off_i = twice * real, twice * imag
        cc = cosine * cosine
        oo = off_r * off_r + off_i * off_i
        cross = (cosine + cosine) * (off_r * real + off_i * imag)
        new_dt.append(cc * at + oo * ab - cross)
        new_db.append(cc * ab + oo * at + cross)
        new_top.append(
            (
                cosine * zt - off_r * zb - off_i * izb,
                cosine * izt - off_r * izb + off_i * zb,
                cosine * xt - off_r * xb - off_i * ixb,
                cosine * ixt - off_r * ixb + off_i * xb,
            )
        )
        new_bottom.append(
            (
                cosine * zb + off_r * zt - off_i * izt,
                cosine * izb + off_r * izt + off_i * zt,
                cosine * xb + off_r * xt - off_i * ixt,
                cosine * ixb + off_r * ixt + off_i * xt,
            )
        )
    return new_top, new_bottom, new_dt, new_db


def advance(state):
    top, bottom, diag_t, diag_b = state
    row = lax.broadcasted_iota(jnp.int32, (8, LANES), 0)

    def ring(tops, bottoms):
        last = jnp.where(row == 7, bottoms[3], pltpu.roll(tops[0], 7, 0))
        first = jnp.where(row == 0, bottoms[0], pltpu.roll(bottoms[3], 1, 0))
        second = jnp.where(row == 0, tops[0], bottoms[0])
        return [tops[1], tops[2], tops[3], last], [first, second, bottoms[1], bottoms[2]]

    parts = [ring([t[i] for t in top], [b[i] for b in bottom]) for i in range(4)]
    new_top = [tuple(parts[i][0][v] for i in range(4)) for v in range(GROUPS)]
    new_bottom = [tuple(parts[i][1][v] for i in range(4)) for v in range(GROUPS)]
    new_dt, new_db = ring(diag_t, diag_b)
    return new_top, new_bottom, new_dt, new_db


def modes_kernel(gram_ref, q_ref, lam_ref, modes_ref, rows_ref):
    lane = lax.broadcasted_iota(jnp.int32, (8, LANES), 1)
    sub = lax.broadcasted_iota(jnp.int32, (8, LANES), 0)
    for v in range(GROUPS):
        for s in range(8):
            p = GROUPS * s + v
            rows_ref[8 * v + s : 8 * v + s + 1, :] = gram_ref[p : p + 1, :]
            rows_ref[32 + 8 * v + s : 33 + 8 * v + s, :] = gram_ref[63 - p : 64 - p, :]
    flip = jnp.where(lane < NB, -1.0, 1.0)
    top, bottom, diag_t, diag_b, ranks = [], [], [], [], []
    for v in range(GROUPS):
        p = GROUPS * sub + v
        for base, index, rows, diag in ((0, p, top, diag_t), (32, 63 - p, bottom, diag_b)):
            z = rows_ref[base + 8 * v : base + 8 * v + 8, :]
            x = jnp.where(lane == index, 1.0, 0.0)
            ix = jnp.where(lane == index + NB, 1.0, 0.0)
            rows.append((z, flip * pltpu.roll(z, NB, 1), x, ix))
            diag.append(jnp.broadcast_to(jnp.sum(z * x, axis=1, keepdims=True), (8, LANES)))
        ranks.append(jnp.where(p == 0, 1000, p))
    flat, tree = jax.tree.flatten((top, bottom, diag_t, diag_b))

    def some_rounds(step, flat):
        state = jax.tree.unflatten(tree, flat)
        base = lax.rem(step * UNROLL, NB - 1)
        for i in range(UNROLL):
            offset = 31 - jnp.abs(base + i - 31)
            state = advance(rotate(state, offset, ranks))
        return jax.tree.flatten(state)[0]

    flat = lax.fori_loop(0, SWEEPS * (NB - 1) // UNROLL, some_rounds, flat)
    top, bottom, diag_t, diag_b = jax.tree.unflatten(tree, flat)
    for v in range(GROUPS):
        for rows, diag, low in ((top[v], diag_t[v], True), (bottom[v], diag_b[v], False)):
            x, ix = rows[2], rows[3]
            left = lane < NB
            sum_real = jnp.sum(jnp.where(left, x, 0.0), axis=1, keepdims=True)
            sum_imag = -jnp.sum(jnp.where(left, 0.0, x), axis=1, keepdims=True)
            magnitude = jnp.sqrt(sum_real * sum_real + sum_imag * sum_imag)
            scaling = 1.0 / (jnp.maximum(magnitude, 1.0) * jnp.sqrt(NB * (diag + 1e-06)))
            phase_r, phase_i = sum_real * scaling, -sum_imag * scaling
            coef = jnp.where(left, 1.0, -1.0) * (x * phase_r - ix * phase_i)
            for s in range(8):
                p = GROUPS * s + v
                row = p if low else 63 - p
                rows_ref[row : row + 1, :] = coef[s : s + 1, :]
                lam_ref[row : row + 1, :] = diag[s : s + 1, :]
    nparts = q_ref.shape[0] // NB
    coefs = rows_ref[...]
    lhs = jnp.concatenate([coefs[:, :NB], coefs[:, NB:]], 0)
    for v in range(nparts // 2):
        real = q_ref[pl.ds(2 * v, NB, stride=nparts), :]
        imag = q_ref[pl.ds(2 * v + 1, NB, stride=nparts), :]
        out = jnp.dot(lhs, jnp.concatenate([real, imag], 1), precision=HIGH, preferred_element_type=F32)
        modes_ref[pl.ds(2 * v, NB, stride=nparts), :] = out[:NB, :LANES] - out[NB:, LANES:]
        modes_ref[pl.ds(2 * v + 1, NB, stride=nparts), :] = out[:NB, LANES:] + out[NB:, :LANES]


def spec(space):
    return pl.BlockSpec(memory_space=space)


def summed(part, axis):
    size = lax.axis_size(axis)
    step = 1
    while step < size:
        part = part + lax.ppermute(part, axis, [(i, i ^ step) for i in range(size)])
        step *= 2
    return part


def body(snapshots, weights, offsets, freqs):
    nfft, nvars, npts = snapshots.shape
    nfreq = freqs.shape[0]
    nblocks = lax.axis_size("blk")
    total_pts = npts * lax.axis_size("pts")
    block = lax.axis_index("blk").astype(jnp.int32).reshape(1)
    own = jnp.transpose(snapshots, (1, 0, 2))
    route = [(i + 1, i) for i in range(nblocks - 1)]
    following = lax.ppermute(own, "blk", route)
    table = pl.pallas_call(
        table_kernel,
        out_shape=jax.ShapeDtypeStruct((2 * nfreq, nfft), F32),
        in_specs=[spec(pltpu.SMEM), spec(pltpu.SMEM), spec(pltpu.VMEM)],
        compiler_params=PARAMS,
        name="table",
    )(block, offsets, freqs.reshape(nfreq, 1))
    scale = 1.0 / (nblocks * nvars * total_pts)
    spectra, energy = pl.pallas_call(
        functools.partial(spectra_kernel, scale),
        out_shape=[
            jax.ShapeDtypeStruct((nfreq * 2 * nvars, npts), F32),
            jax.ShapeDtypeStruct((8, npts), F32),
        ],
        in_specs=[spec(pltpu.SMEM), spec(pltpu.SMEM)] + [spec(pltpu.VMEM)] * 4,
        compiler_params=PARAMS,
        name="spectra",
    )(block, offsets, table, own, following, weights)
    energies = lax.all_gather(energy, ("blk", "pts"), axis=0, tiled=True)
    grouped = lax.all_to_all(
        spectra.reshape(nfreq, 1, nvars, 2, npts), "blk", split_axis=0, concat_axis=1, tiled=True
    ).reshape(nblocks * 2 * nvars, npts)
    gram = pl.pallas_call(
        functools.partial(gram_kernel, scale),
        out_shape=jax.ShapeDtypeStruct((nblocks, 2 * nblocks), F32),
        compiler_params=PARAMS,
        name="gram",
    )(grouped, weights)
    gram = summed(gram, "pts")
    lam, modes = pl.pallas_call(
        modes_kernel,
        out_shape=[
            jax.ShapeDtypeStruct((nblocks, LANES), F32),
            jax.ShapeDtypeStruct((nblocks * 2 * nvars, npts), F32),
        ],
        scratch_shapes=[pltpu.VMEM((nblocks, LANES), F32)],
        compiler_params=PARAMS,
        name="modes",
    )(gram, grouped)
    eigen = lam[:, 0].reshape(1, nblocks)
    total = jnp.sum(energies)
    modes = modes.reshape(1, nblocks, nvars, 2, npts).transpose(0, 1, 3, 2, 4)
    return modes, nfreq * nblocks * eigen / total


def solution(mesh):
    return jax.shard_map(
        body,
        mesh=mesh,
        in_specs=(P("blk", None, "pts"), P(None, "pts"), P(), P()),
        out_specs=(P("blk", None, None, None, "pts"), P("blk", None)),
        check_vma=False,
    )
```

```python
import functools
import math

import jax
import jax.numpy as jnp
from jax import lax
from jax.experimental import pallas as pl
from jax.experimental.pallas import tpu as pltpu
from jax.sharding import PartitionSpec as P

SWEEPS = 2
HIGH = lax.Precision.HIGHEST
DAMPING = 0.01
F32 = jnp.float32
NFFT = 256
NB = 64
LANES = 128
GROUPS = 4
UNROLL = 7
PARAMS = pltpu.CompilerParams(vmem_limit_bytes=16 << 20)


def half_spectra_kernel(tail, nvars, place_ref, offsets_ref, freqs_ref, own_ref, out_ref, data_ref, sem):
    copies = [pltpu.make_async_copy(own_ref.at[v], data_ref.at[v], sem.at[v]) for v in range(nvars)]
    for copy in copies:
        copy.start()
    block = place_ref[0]
    offset = offsets_ref[jnp.maximum(block - 1, 0) if tail else block]
    snapshot = lax.broadcasted_iota(jnp.int32, (1, NFFT), 1)
    lag = jnp.bitwise_and(snapshot - offset, NFFT - 1)
    valid = snapshot < offset if tail else snapshot >= offset
    unit = 2.0 * math.pi / NFFT
    hann = jnp.where(valid, 0.5 - 0.5 * jnp.cos(unit * lag.astype(F32)), 0.0) / math.sqrt(NFFT)
    square = (NB, NB)
    same = lax.broadcasted_iota(jnp.int32, square, 0) == lax.broadcasted_iota(jnp.int32, square, 1)
    freqs = jnp.sum(jnp.where(same, freqs_ref[...].astype(F32), 0.0), axis=1, keepdims=True).astype(jnp.int32)
    angle = unit * jnp.bitwise_and(freqs * lag, NFFT - 1).astype(F32)
    table = jnp.concatenate([hann * jnp.cos(angle), -hann * jnp.sin(angle)], 0)
    for v in range(nvars):
        copies[v].wait()
        result = jnp.dot(table, data_ref[v], precision=HIGH, preferred_element_type=F32)
        for part in range(2):
            out_ref[pl.ds(2 * v + part, NB, stride=2 * nvars), :] = result[part * NB : (part + 1) * NB]


def join_kernel(scale, head_ref, tail_ref, weights_ref, out_ref):
    nvars = weights_ref.shape[0]
    rows = 2 * nvars + 1
    energy = jnp.zeros((1, LANES), F32)
    for j in range(2 * nvars):
        value = head_ref[pl.ds(j, NB, stride=2 * nvars), :] + tail_ref[pl.ds(j, NB, stride=2 * nvars), :]
        out_ref[pl.ds(j, NB, stride=rows), :] = value
        weight = weights_ref[j // 2 : j // 2 + 1, :] * scale
        energy = energy + jnp.sum(value * value, axis=0, keepdims=True) * weight
    out_ref[pl.ds(rows - 1, NB, stride=rows), :] = jnp.broadcast_to(energy, (NB, LANES))


def gram_kernel(scale, copies, q_ref, weights_ref, out_ref):
    nvars = weights_ref.shape[0]
    rows = 2 * nvars + 1
    left, right_real, right_imag = [], [], []
    for v in range(nvars):
        real = q_ref[pl.ds(2 * v, NB, stride=rows), :]
        imag = q_ref[pl.ds(2 * v + 1, NB, stride=rows), :]
        weight = weights_ref[v : v + 1, :] * scale
        left += [real * weight, imag * weight]
        right_real += [real, imag]
        right_imag += [imag, -real]
    right = jnp.concatenate([jnp.concatenate(right_real, 1), jnp.concatenate(right_imag, 1)], 0)
    gram = lax.dot_general(
        jnp.concatenate(left, 1), right, (((1,), (1,)), ((), ())), precision=HIGH, preferred_element_type=F32
    )
    row, lane = (lax.broadcasted_iota(jnp.int32, (NB, LANES), d) for d in range(2))
    mixed = jnp.where(lane >= row, gram, pltpu.roll(gram, NB, 1))
    half = NB // 2
    packed = jnp.where(lane[:half] < NB, mixed[:half], pltpu.roll(mixed[half:], NB, 1))
    energy = jnp.sum(q_ref[pl.ds(rows - 1, NB, stride=rows), :], axis=0, keepdims=True)
    energy = jnp.where(row[:8] == 0, energy, 0.0)
    for k in range(copies):
        out_ref[k, :half, :] = packed
        out_ref[k, half:, :] = energy


def unpacked(parts_ref):
    total = parts_ref[0]
    for k in range(1, parts_ref.shape[0]):
        total = total + parts_ref[k]
    half = NB // 2
    packed = total[:half]
    row, lane = (lax.broadcasted_iota(jnp.int32, (NB, LANES), d) for d in range(2))
    mixed = jnp.concatenate([packed, pltpu.roll(packed, NB, 1)], 0)
    turned = jnp.transpose(jnp.concatenate([mixed, jnp.zeros_like(mixed)], 0))[:NB]
    real = jnp.where(lane >= row, mixed, turned)
    imag = jnp.where(lane < row, mixed, jnp.where(lane > row, -turned, 0.0))
    return jnp.where(lane < NB, real, pltpu.roll(imag, NB, 1)), jnp.sum(total[half : half + 1], axis=1, keepdims=True)


def rotate(state, offset, ranks):
    top, bottom, diag_t, diag_b = state
    new_top, new_bottom, new_dt, new_db = [], [], [], []
    for v in range(GROUPS):
        zt, izt, xt, ixt = top[v]
        zb, izb, xb, ixb = bottom[v]
        real = jnp.sum(zt * xb, axis=1, keepdims=True)
        imag = jnp.sum(zt * ixb, axis=1, keepdims=True)
        at, ab = diag_t[v], diag_b[v]
        sign = jnp.where(ranks[v] > offset, 1.0, -1.0)
        delta = sign * (ab - at)
        four = 4.0 * (real * real + imag * imag)
        square = delta * delta + four
        radius = square * lax.rsqrt(jnp.maximum(square, 1e-37))
        upper = radius + delta + DAMPING * (ab + at)
        inverse = lax.rsqrt(upper * upper + four)
        cosine = upper * inverse
        twice = (sign + sign) * inverse
        off_r, off_i = twice * real, twice * imag
        cc = cosine * cosine
        oo = off_r * off_r + off_i * off_i
        cross = (cosine + cosine) * (off_r * real + off_i * imag)
        new_dt.append(cc * at + oo * ab - cross)
        new_db.append(cc * ab + oo * at + cross)
        new_top.append(
            (
                cosine * zt - off_r * zb - off_i * izb,
                cosine * izt - off_r * izb + off_i * zb,
                cosine * xt - off_r * xb - off_i * ixb,
                cosine * ixt - off_r * ixb + off_i * xb,
            )
        )
        new_bottom.append(
            (
                cosine * zb + off_r * zt - off_i * izt,
                cosine * izb + off_r * izt + off_i * zt,
                cosine * xb + off_r * xt - off_i * ixt,
                cosine * ixb + off_r * ixt + off_i * xt,
            )
        )
    return new_top, new_bottom, new_dt, new_db


def advance(state):
    top, bottom, diag_t, diag_b = state
    row = lax.broadcasted_iota(jnp.int32, (8, LANES), 0)

    def ring(tops, bottoms):
        last = jnp.where(row == 7, bottoms[3], pltpu.roll(tops[0], 7, 0))
        first = jnp.where(row == 0, bottoms[0], pltpu.roll(bottoms[3], 1, 0))
        second = jnp.where(row == 0, tops[0], bottoms[0])
        return [tops[1], tops[2], tops[3], last], [first, second, bottoms[1], bottoms[2]]

    parts = [ring([t[i] for t in top], [b[i] for b in bottom]) for i in range(4)]
    new_top = [tuple(parts[i][0][v] for i in range(4)) for v in range(GROUPS)]
    new_bottom = [tuple(parts[i][1][v] for i in range(4)) for v in range(GROUPS)]
    new_dt, new_db = ring(diag_t, diag_b)
    return new_top, new_bottom, new_dt, new_db


def modes_kernel(parts_ref, q_ref, modes_ref, spectrum_ref, gram_ref, rows_ref):
    lane = lax.broadcasted_iota(jnp.int32, (8, LANES), 1)
    sub = lax.broadcasted_iota(jnp.int32, (8, LANES), 0)
    gram_ref[...], energy = unpacked(parts_ref)
    for v in range(GROUPS):
        for s in range(8):
            p = GROUPS * s + v
            rows_ref[8 * v + s : 8 * v + s + 1, :] = gram_ref[p : p + 1, :]
            rows_ref[32 + 8 * v + s : 33 + 8 * v + s, :] = gram_ref[63 - p : 64 - p, :]
    flip = jnp.where(lane < NB, -1.0, 1.0)
    top, bottom, diag_t, diag_b, ranks = [], [], [], [], []
    for v in range(GROUPS):
        p = GROUPS * sub + v
        for base, index, rows, diag in ((0, p, top, diag_t), (32, 63 - p, bottom, diag_b)):
            z = rows_ref[base + 8 * v : base + 8 * v + 8, :]
            x = jnp.where(lane == index, 1.0, 0.0)
            ix = jnp.where(lane == index + NB, 1.0, 0.0)
            rows.append((z, flip * pltpu.roll(z, NB, 1), x, ix))
            diag.append(jnp.broadcast_to(jnp.sum(z * x, axis=1, keepdims=True), (8, LANES)))
        ranks.append(jnp.where(p == 0, 1000, p))
    flat, tree = jax.tree.flatten((top, bottom, diag_t, diag_b))

    def some_rounds(step, flat):
        state = jax.tree.unflatten(tree, flat)
        base = lax.rem(step * UNROLL, NB - 1)
        for i in range(UNROLL):
            offset = 31 - jnp.abs(base + i - 31)
            state = advance(rotate(state, offset, ranks))
        return jax.tree.flatten(state)[0]

    flat = lax.fori_loop(0, SWEEPS * (NB - 1) // UNROLL, some_rounds, flat)
    top, bottom, diag_t, diag_b = jax.tree.unflatten(tree, flat)
    eigen = jnp.zeros((8, LANES), F32)
    left = lane < NB
    for v in range(GROUPS):
        for rows, diag, low in ((top[v], diag_t[v], True), (bottom[v], diag_b[v], False)):
            x, ix = rows[2], rows[3]
            sum_real = jnp.sum(jnp.where(left, x, 0.0), axis=1, keepdims=True)
            sum_imag = -jnp.sum(jnp.where(left, 0.0, x), axis=1, keepdims=True)
            magnitude = jnp.sqrt(sum_real * sum_real + sum_imag * sum_imag)
            scaling = 1.0 / (jnp.maximum(magnitude, 1.0) * jnp.sqrt(NB * (diag + 1e-06)))
            phase_r, phase_i = sum_real * scaling, -sum_imag * scaling
            coef = jnp.where(left, 1.0, -1.0) * (x * phase_r - ix * phase_i)
            index = GROUPS * sub + v if low else 63 - GROUPS * sub - v
            eigen = eigen + jnp.where(lane == index, diag, 0.0)
            for s in range(8):
                p = GROUPS * s + v
                row = p if low else 63 - p
                rows_ref[row : row + 1, :] = coef[s : s + 1, :]
    spectrum = jnp.sum(eigen, axis=0, keepdims=True) * (NB * NB) / energy
    spectrum_ref[...] = spectrum[:, :NB]
    rows = q_ref.shape[0] // NB
    nparts = rows - 1
    coefs = rows_ref[...]
    lhs = jnp.concatenate([coefs[:, :NB], coefs[:, NB:]], 0)
    for v in range(nparts // 2):
        real = q_ref[pl.ds(2 * v, NB, stride=rows), :]
        imag = q_ref[pl.ds(2 * v + 1, NB, stride=rows), :]
        out = jnp.dot(lhs, jnp.concatenate([real, imag], 1), precision=HIGH, preferred_element_type=F32)
        modes_ref[pl.ds(2 * v, NB, stride=nparts), :] = out[:NB, :LANES] - out[NB:, LANES:]
        modes_ref[pl.ds(2 * v + 1, NB, stride=nparts), :] = out[:NB, LANES:] + out[NB:, :LANES]


def spec(space):
    return pl.BlockSpec(memory_space=space)


def half_spectra(tail, place, offsets, freqs, own):
    nvars, nfft, npts = own.shape
    return pl.pallas_call(
        functools.partial(half_spectra_kernel, tail, nvars),
        out_shape=jax.ShapeDtypeStruct((NB * 2 * nvars, npts), F32),
        in_specs=[spec(pltpu.SMEM), spec(pltpu.SMEM), spec(pltpu.VMEM), spec(pltpu.HBM)],
        scratch_shapes=[pltpu.VMEM((nvars, nfft, npts), F32), pltpu.SemaphoreType.DMA((nvars,))],
        compiler_params=PARAMS,
        cost_estimate=pl.CostEstimate(flops=12 * NB * 2 * nfft * nvars * npts, bytes_accessed=4 * own.size, transcendentals=0),
        name="tail" if tail else "head",
    )(place, offsets, freqs, own)


def body(snapshots, weights, offsets, freqs):
    nfft, nvars, npts = snapshots.shape
    nfreq = freqs.shape[0]
    nblocks = lax.axis_size("blk")
    nparts = lax.axis_size("pts")
    rows = 2 * nvars + 1
    place = lax.axis_index("blk").astype(jnp.int32).reshape(1)
    own = jnp.transpose(snapshots, (1, 0, 2))
    freqs = freqs.reshape(1, nfreq)
    tail = half_spectra(True, place, offsets, freqs, own)
    tail = lax.ppermute(tail, "blk", [(i + 1, i) for i in range(nblocks - 1)])
    head = half_spectra(False, place, offsets, freqs, own)
    scale = 1.0 / (nblocks * nvars * npts * nparts)
    spectra = pl.pallas_call(
        functools.partial(join_kernel, scale),
        out_shape=jax.ShapeDtypeStruct((nfreq * rows, npts), F32),
        compiler_params=PARAMS,
        name="join",
    )(head, tail, weights)
    grouped = lax.all_to_all(
        spectra.reshape(nfreq, 1, rows, 1, npts), "blk", split_axis=0, concat_axis=1, tiled=True
    ).reshape(nblocks * rows, npts)
    gram = pl.pallas_call(
        functools.partial(gram_kernel, scale, nparts),
        out_shape=jax.ShapeDtypeStruct((nparts, nblocks // 2 + 8, LANES), F32),
        compiler_params=PARAMS,
        name="gram",
    )(grouped, weights)
    parts = lax.all_to_all(gram, "pts", split_axis=0, concat_axis=0, tiled=True)
    modes, spectrum = pl.pallas_call(
        modes_kernel,
        out_shape=[
            jax.ShapeDtypeStruct((nblocks * 2 * nvars, npts), F32),
            jax.ShapeDtypeStruct((1, nblocks), F32),
        ],
        scratch_shapes=[pltpu.VMEM((nblocks, LANES), F32)] * 2,
        compiler_params=PARAMS,
        name="modes",
    )(parts, grouped)
    modes = modes.reshape(1, nblocks, nvars, 2, npts).transpose(0, 1, 3, 2, 4)
    return modes, spectrum


def solution(mesh):
    return jax.shard_map(
        body,
        mesh=mesh,
        in_specs=(P("blk", None, "pts"), P(None, "pts"), P(), P()),
        out_specs=(P("blk", None, None, None, "pts"), P("blk", None)),
        check_vma=False,
    )
```

```python
import functools
import math

import jax
import jax.numpy as jnp
from jax import lax
from jax.experimental import pallas as pl
from jax.experimental.pallas import tpu as pltpu
from jax.sharding import PartitionSpec as P

SWEEPS = 2
HIGH = lax.Precision.HIGHEST
DAMPING = 0.01
F32 = jnp.float32
NFFT = 256
NB = 64
LANES = 128
GROUPS = 4
UNROLL = 7
PARAMS = pltpu.CompilerParams(vmem_limit_bytes=16 << 20)


def half_spectra_kernel(tail, nvars, offsets_hbm, freqs_hbm, own_ref, out_ref, offsets_ref, freqs_ref, data_ref, sem):
    small = [
        pltpu.make_async_copy(offsets_hbm, offsets_ref, sem.at[nvars]),
        pltpu.make_async_copy(freqs_hbm, freqs_ref, sem.at[nvars + 1]),
    ]
    copies = [pltpu.make_async_copy(own_ref.at[v], data_ref.at[v], sem.at[v]) for v in range(nvars)]
    for copy in small + copies:
        copy.start()
    block = lax.axis_index("blk")
    if tail:
        block = jnp.where(block == 0, NB, block) - 1
    for copy in small:
        copy.wait()
    offset = offsets_ref[0, block]
    snapshot = lax.broadcasted_iota(jnp.int32, (1, NFFT), 1)
    lag = jnp.bitwise_and(snapshot - offset, NFFT - 1)
    valid = snapshot < offset if tail else snapshot >= offset
    unit = 2.0 * math.pi / NFFT
    hann = jnp.where(valid, 0.5 - 0.5 * jnp.cos(unit * lag.astype(F32)), 0.0) / math.sqrt(NFFT)
    square = (NB, NB)
    same = lax.broadcasted_iota(jnp.int32, square, 0) == lax.broadcasted_iota(jnp.int32, square, 1)
    freqs = jnp.sum(jnp.where(same, freqs_ref[...].astype(F32), 0.0), axis=1, keepdims=True).astype(jnp.int32)
    angle = unit * jnp.bitwise_and(freqs * lag, NFFT - 1).astype(F32)
    table = jnp.concatenate([hann * jnp.cos(angle), -hann * jnp.sin(angle)], 0)
    for copy in copies:
        copy.wait()
    data = jnp.concatenate([data_ref[v] for v in range(nvars)], 1)
    result = jnp.dot(table, data, precision=HIGH, preferred_element_type=F32)
    for v in range(nvars):
        for part in range(2):
            piece = result[part * NB : (part + 1) * NB, v * LANES : (v + 1) * LANES]
            out_ref[pl.ds(2 * v + part, NB, stride=2 * nvars), :] = piece


def join_kernel(scale, head_ref, tail_ref, weights_ref, out_ref):
    nvars = weights_ref.shape[0]
    rows = 2 * nvars + 1
    energy = jnp.zeros((1, LANES), F32)
    for j in range(2 * nvars):
        value = head_ref[pl.ds(j, NB, stride=2 * nvars), :] + tail_ref[pl.ds(j, NB, stride=2 * nvars), :]
        out_ref[pl.ds(j, NB, stride=rows), :] = value
        weight = weights_ref[j // 2 : j // 2 + 1, :] * scale
        energy = energy + jnp.sum(value * value, axis=0, keepdims=True) * weight
    out_ref[pl.ds(rows - 1, NB, stride=rows), :] = jnp.broadcast_to(energy, (NB, LANES))


def gram_kernel(scale, copies, q_ref, weights_ref, out_ref):
    nvars = weights_ref.shape[0]
    rows = 2 * nvars + 1
    left, right_real, right_imag = [], [], []
    for v in range(nvars):
        real = q_ref[pl.ds(2 * v, NB, stride=rows), :]
        imag = q_ref[pl.ds(2 * v + 1, NB, stride=rows), :]
        weight = weights_ref[v : v + 1, :] * scale
        left += [real * weight, imag * weight]
        right_real += [real, imag]
        right_imag += [imag, -real]
    right = jnp.concatenate([jnp.concatenate(right_real, 1), jnp.concatenate(right_imag, 1)], 0)
    gram = lax.dot_general(
        jnp.concatenate(left, 1), right, (((1,), (1,)), ((), ())), precision=HIGH, preferred_element_type=F32
    )
    row, lane = (lax.broadcasted_iota(jnp.int32, (NB, LANES), d) for d in range(2))
    mixed = jnp.where(lane >= row, gram, pltpu.roll(gram, NB, 1))
    half = NB // 2
    packed = jnp.where(lane[:half] < NB, mixed[:half], pltpu.roll(mixed[half:], NB, 1))
    energy = jnp.sum(q_ref[pl.ds(rows - 1, NB, stride=rows), :], axis=0, keepdims=True)
    energy = jnp.where(row[:8] == 0, energy, 0.0)
    for k in range(copies):
        out_ref[k, :half, :] = packed
        out_ref[k, half:, :] = energy


def unpacked(parts_ref):
    total = parts_ref[0]
    for k in range(1, parts_ref.shape[0]):
        total = total + parts_ref[k]
    half = NB // 2
    packed = total[:half]
    row, lane = (lax.broadcasted_iota(jnp.int32, (NB, LANES), d) for d in range(2))
    mixed = jnp.concatenate([packed, pltpu.roll(packed, NB, 1)], 0)
    turned = jnp.transpose(jnp.concatenate([mixed, jnp.zeros_like(mixed)], 0))[:NB]
    real = jnp.where(lane >= row, mixed, turned)
    imag = jnp.where(lane < row, mixed, jnp.where(lane > row, -turned, 0.0))
    return jnp.where(lane < NB, real, pltpu.roll(imag, NB, 1)), jnp.sum(total[half : half + 1], axis=1, keepdims=True)


def shift_top(tops, bottoms, row):
    return [tops[1], tops[2], tops[3], jnp.where(row == 7, bottoms, pltpu.roll(tops[0], 7, 0))]


def shift_bottom(tops, bottoms, row):
    first = jnp.where(row == 0, bottoms[0], pltpu.roll(bottoms[3], 1, 0))
    second = bottoms[0] if tops is None else jnp.where(row == 0, tops, bottoms[0])
    return [first, second, bottoms[1], bottoms[2]]


def one_round(state, offset, ranks, row):
    top, bottom, diag_t, diag_b, beta = state

    def col(rows, i):
        return [r[i] for r in rows]

    total = lambda x: jnp.sum(x, axis=1, keepdims=True)
    tz, bz = col(top, 0), col(bottom, 0)
    uz, wz = shift_top(tz, bz[3], row), shift_top(bz, tz[3], row)
    ux, uix, wx, wix = [], [], [], []
    for i, (u, w) in ((2, (ux, wx)), (3, (uix, wix))):
        t, b = col(top, i), col(bottom, i)
        u += shift_bottom(t[0], b, row)
        w += shift_bottom(b[0], t, row)
    inner = []
    for v in range(GROUPS):
        inner.append([(total(z * x), total(z * ix)) for z in (uz[v], wz[v]) for x, ix in ((ux[v], uix[v]), (wx[v], wix[v]))])
    cos, off, img, new_dt, new_db = [], [], [], [], []
    wide = lambda x: jnp.broadcast_to(x, (8, LANES))
    new_top, new_bottom = [], []
    for v in range(GROUPS):
        real, imag = beta[v]
        at, ab = diag_t[v], diag_b[v]
        sign = jnp.where(ranks[v] > offset, 1.0, -1.0)
        gap = ab - at
        delta = sign * gap
        four = 4.0 * (real * real + imag * imag)
        square = delta * delta + four
        radius = square * lax.rsqrt(jnp.maximum(square, 1e-37))
        upper = radius + (delta + DAMPING * (ab + at))
        inverse = lax.rsqrt(upper * upper + four)
        c = upper * inverse
        twice = (sign + sign) * inverse
        r, i = twice * real, twice * imag
        moved = (four * inverse) * (inverse * gap - sign * c)
        new_dt.append(at + moved)
        new_db.append(ab - moved)
        cos.append(c); off.append(r); img.append(i)
        (zt, izt, xt, ixt), (zb, izb, xb, ixb) = top[v], bottom[v]
        new_top.append((c * zt - r * zb - i * izb, c * izt - r * izb + i * zb, c * xt - r * xb - i * ixb, c * ixt - r * ixb + i * xb))
        new_bottom.append((c * zb + r * zt - i * izt, c * izb + r * izt + i * zt, c * xb + r * xt - i * ixt, c * ixb + r * ixt + i * xt))
    c1, r1, i1 = shift_top(cos, cos[3], row), shift_top(off, -off[3], row), shift_top(img, img[3], row)
    c2, r2, i2 = shift_bottom(None, cos, row), shift_bottom(-off[0], off, row), shift_bottom(None, img, row)
    new_beta = []
    for v in range(GROUPS):
        uu, uw, wu, ww = inner[v]
        ca, ra, ia, cb, rb, ib = c1[v], r1[v], i1[v], c2[v], r2[v], i2[v]
        ur = cb * uu[0] + rb * uw[0] - ib * uw[1]
        ui = cb * uu[1] + rb * uw[1] + ib * uw[0]
        wr = cb * wu[0] + rb * ww[0] - ib * ww[1]
        wi = cb * wu[1] + rb * ww[1] + ib * ww[0]
        new_beta.append((wide(ca * ur - ra * wr + ia * wi), wide(ca * ui - ra * wi - ia * wr)))
    tops = [shift_top(col(new_top, i), new_bottom[3][i], row) for i in range(4)]
    bottoms = [shift_bottom(new_top[0][i], col(new_bottom, i), row) for i in range(4)]
    return (list(zip(*tops)), list(zip(*bottoms)), shift_top(new_dt, new_db[3], row),
            shift_bottom(new_dt[0], new_db, row), new_beta)


def modes_kernel(parts_ref, q_ref, modes_ref, spectrum_ref, gram_ref, rows_ref):
    lane = lax.broadcasted_iota(jnp.int32, (8, LANES), 1)
    sub = lax.broadcasted_iota(jnp.int32, (8, LANES), 0)
    gram_ref[...], energy = unpacked(parts_ref)
    for v in range(GROUPS):
        for s in range(8):
            p = GROUPS * s + v
            rows_ref[8 * v + s : 8 * v + s + 1, :] = gram_ref[p : p + 1, :]
            rows_ref[32 + 8 * v + s : 33 + 8 * v + s, :] = gram_ref[63 - p : 64 - p, :]
    flip = jnp.where(lane < NB, -1.0, 1.0)
    top, bottom, diag_t, diag_b, ranks = [], [], [], [], []
    for v in range(GROUPS):
        p = GROUPS * sub + v
        for base, index, rows, diag in ((0, p, top, diag_t), (32, 63 - p, bottom, diag_b)):
            z = rows_ref[base + 8 * v : base + 8 * v + 8, :]
            x = jnp.where(lane == index, 1.0, 0.0)
            ix = jnp.where(lane == index + NB, 1.0, 0.0)
            rows.append((z, flip * pltpu.roll(z, NB, 1), x, ix))
            diag.append(jnp.broadcast_to(jnp.sum(z * x, axis=1, keepdims=True), (8, LANES)))
        ranks.append(jnp.where(p == 0, 1000, p))
    def inner(z, x):
        return jnp.broadcast_to(jnp.sum(z * x, axis=1, keepdims=True), (8, LANES))

    beta = [(inner(t[0], b[2]), inner(t[0], b[3])) for t, b in zip(top, bottom)]
    flat, tree = jax.tree.flatten((top, bottom, diag_t, diag_b, beta))

    def some_rounds(step, flat):
        state = jax.tree.unflatten(tree, flat)
        base = lax.rem(step * UNROLL, NB - 1)
        for i in range(UNROLL):
            offset = 31 - jnp.abs(base + i - 31)
            state = one_round(state, offset, ranks, sub)
        return jax.tree.flatten(state)[0]

    flat = lax.fori_loop(0, SWEEPS * (NB - 1) // UNROLL, some_rounds, flat)
    top, bottom, diag_t, diag_b, _ = jax.tree.unflatten(tree, flat)
    eigen = jnp.zeros((8, LANES), F32)
    left = lane < NB
    for v in range(GROUPS):
        for rows, diag, low in ((top[v], diag_t[v], True), (bottom[v], diag_b[v], False)):
            x, ix = rows[2], rows[3]
            sum_real = jnp.sum(jnp.where(left, x, 0.0), axis=1, keepdims=True)
            sum_imag = -jnp.sum(jnp.where(left, 0.0, x), axis=1, keepdims=True)
            magnitude = jnp.sqrt(sum_real * sum_real + sum_imag * sum_imag)
            scaling = 1.0 / (jnp.maximum(magnitude, 1.0) * jnp.sqrt(NB * (diag + 1e-06)))
            phase_r, phase_i = sum_real * scaling, -sum_imag * scaling
            coef = jnp.where(left, 1.0, -1.0) * (x * phase_r - ix * phase_i)
            index = GROUPS * sub + v if low else 63 - GROUPS * sub - v
            eigen = eigen + jnp.where(lane == index, diag, 0.0)
            for s in range(8):
                p = GROUPS * s + v
                row = p if low else 63 - p
                rows_ref[row : row + 1, :] = coef[s : s + 1, :]
    spectrum = jnp.sum(eigen, axis=0, keepdims=True) * (NB * NB) / energy
    spectrum_ref[...] = spectrum[:, :NB]
    rows = q_ref.shape[0] // NB
    nparts = rows - 1
    coefs = rows_ref[...]
    lhs = jnp.concatenate([coefs[:, :NB], coefs[:, NB:]], 0)
    for v in range(nparts // 2):
        real = q_ref[pl.ds(2 * v, NB, stride=rows), :]
        imag = q_ref[pl.ds(2 * v + 1, NB, stride=rows), :]
        out = jnp.dot(lhs, jnp.concatenate([real, imag], 1), precision=HIGH, preferred_element_type=F32)
        modes_ref[pl.ds(2 * v, NB, stride=nparts), :] = out[:NB, :LANES] - out[NB:, LANES:]
        modes_ref[pl.ds(2 * v + 1, NB, stride=nparts), :] = out[:NB, LANES:] + out[NB:, :LANES]


def spec(space):
    return pl.BlockSpec(memory_space=space)


def half_spectra(tail, offsets, freqs, own):
    nvars, nfft, npts = own.shape
    return pl.pallas_call(
        functools.partial(half_spectra_kernel, tail, nvars),
        out_shape=jax.ShapeDtypeStruct((NB * 2 * nvars, npts), F32),
        in_specs=[spec(pl.ANY)] * 3,
        scratch_shapes=[
            pltpu.SMEM(offsets.shape, jnp.int32),
            pltpu.VMEM(freqs.shape, jnp.int32),
            pltpu.VMEM((nvars, nfft, npts), F32),
            pltpu.SemaphoreType.DMA((nvars + 2,)),
        ],
        compiler_params=pltpu.CompilerParams(vmem_limit_bytes=(60 if tail else 16) << 20),
        cost_estimate=pl.CostEstimate(flops=12 * NB * 2 * nfft * nvars * npts, bytes_accessed=4 * own.size, transcendentals=0),
        name="tail" if tail else "head",
    )(offsets, freqs, own)


def body(snapshots, weights, offsets, freqs):
    nfft, nvars, npts = snapshots.shape
    nfreq = freqs.shape[0]
    nblocks = lax.axis_size("blk")
    nparts = lax.axis_size("pts")
    rows = 2 * nvars + 1
    own = jnp.transpose(snapshots, (1, 0, 2))
    freqs = freqs.reshape(1, nfreq)
    offsets = offsets.reshape(1, nblocks)
    tail = half_spectra(True, offsets, freqs, own)
    tail = lax.ppermute(tail, "blk", [(i, (i - 1) % nblocks) for i in range(nblocks)])
    head = half_spectra(False, offsets, freqs, own)
    scale = 1.0 / (nblocks * nvars * npts * nparts)
    spectra = pl.pallas_call(
        functools.partial(join_kernel, scale),
        out_shape=jax.ShapeDtypeStruct((nfreq * rows, npts), F32),
        compiler_params=PARAMS,
        name="join",
    )(head, tail, weights)
    grouped = lax.all_to_all(
        spectra.reshape(nfreq, 1, rows, 1, npts), "blk", split_axis=0, concat_axis=1, tiled=True
    ).reshape(nblocks * rows, npts)
    gram = pl.pallas_call(
        functools.partial(gram_kernel, scale, nparts),
        out_shape=jax.ShapeDtypeStruct((nparts, nblocks // 2 + 8, LANES), F32),
        compiler_params=PARAMS,
        name="gram",
    )(grouped, weights)
    parts = lax.all_to_all(gram, "pts", split_axis=0, concat_axis=0, tiled=True)
    modes, spectrum = pl.pallas_call(
        modes_kernel,
        out_shape=[
            jax.ShapeDtypeStruct((nblocks * 2 * nvars, npts), F32),
            jax.ShapeDtypeStruct((1, nblocks), F32),
        ],
        scratch_shapes=[pltpu.VMEM((nblocks, LANES), F32)] * 2,
        compiler_params=PARAMS,
        name="modes",
    )(parts, grouped)
    modes = modes.reshape(1, nblocks, nvars, 2, npts).transpose(0, 1, 3, 2, 4)
    return modes, spectrum


def solution(mesh):
    return jax.shard_map(
        body,
        mesh=mesh,
        in_specs=(P("blk", None, "pts"), P(None, "pts"), P(), P()),
        out_specs=(P("blk", None, None, None, "pts"), P("blk", None)),
        check_vma=False,
    )
```

```python
import functools
import math

import jax
import jax.numpy as jnp
from jax import lax
from jax.experimental import pallas as pl
from jax.experimental.pallas import tpu as pltpu
from jax.sharding import PartitionSpec as P

SWEEPS = 2
HIGH = lax.Precision.HIGHEST
DAMPING = 0.01
F32 = jnp.float32
NFFT = 256
NB = 64
LANES = 128
GROUPS = 4
UNROLL = 20
PARAMS = pltpu.CompilerParams(vmem_limit_bytes=16 << 20)


def half_spectra_kernel(tail, nvars, offsets_hbm, freqs_hbm, own_ref, out_ref, offsets_ref, freqs_ref, data_ref, sem):
    small = [
        pltpu.make_async_copy(offsets_hbm, offsets_ref, sem.at[nvars]),
        pltpu.make_async_copy(freqs_hbm, freqs_ref, sem.at[nvars + 1]),
    ]
    copies = [pltpu.make_async_copy(own_ref.at[v], data_ref.at[v], sem.at[v]) for v in range(nvars)]
    for copy in small + copies:
        copy.start()
    block = lax.axis_index("blk")
    if tail:
        block = jnp.where(block == 0, NB, block) - 1
    for copy in small:
        copy.wait()
    offset = offsets_ref[0, block]
    snapshot = lax.broadcasted_iota(jnp.int32, (1, NFFT), 1)
    lag = jnp.bitwise_and(snapshot - offset, NFFT - 1)
    valid = snapshot < offset if tail else snapshot >= offset
    unit = 2.0 * math.pi / NFFT
    hann = jnp.where(valid, 0.5 - 0.5 * jnp.cos(unit * lag.astype(F32)), 0.0) / math.sqrt(NFFT)
    square = (NB, NB)
    same = lax.broadcasted_iota(jnp.int32, square, 0) == lax.broadcasted_iota(jnp.int32, square, 1)
    freqs = jnp.sum(jnp.where(same, freqs_ref[...].astype(F32), 0.0), axis=1, keepdims=True).astype(jnp.int32)
    angle = unit * jnp.bitwise_and(freqs * lag, NFFT - 1).astype(F32)
    table = jnp.concatenate([hann * jnp.cos(angle), -hann * jnp.sin(angle)], 0)
    for copy in copies:
        copy.wait()
    data = jnp.concatenate([data_ref[v] for v in range(nvars)], 1)
    result = jnp.dot(table, data, precision=HIGH, preferred_element_type=F32)
    for v in range(nvars):
        for part in range(2):
            piece = result[part * NB : (part + 1) * NB, v * LANES : (v + 1) * LANES]
            out_ref[pl.ds(2 * v + part, NB, stride=2 * nvars), :] = piece


def join_kernel(scale, head_ref, tail_ref, weights_ref, out_ref):
    nvars = weights_ref.shape[0]
    rows = 2 * nvars + 1
    energy = jnp.zeros((1, LANES), F32)
    for j in range(2 * nvars):
        value = head_ref[pl.ds(j, NB, stride=2 * nvars), :] + tail_ref[pl.ds(j, NB, stride=2 * nvars), :]
        out_ref[pl.ds(j, NB, stride=rows), :] = value
        weight = weights_ref[j // 2 : j // 2 + 1, :] * scale
        energy = energy + jnp.sum(value * value, axis=0, keepdims=True) * weight
    out_ref[pl.ds(rows - 1, NB, stride=rows), :] = jnp.broadcast_to(energy, (NB, LANES))


def thirds(x):
    high = x.astype(jnp.bfloat16)
    rest = x - high.astype(F32)
    middle = rest.astype(jnp.bfloat16)
    return high, middle, (rest - middle.astype(F32)).astype(jnp.bfloat16)


def gram_kernel(scale, copies, q_ref, weights_ref, out_ref):
    nvars = weights_ref.shape[0]
    rows = 2 * nvars + 1
    left, right_real, right_imag = ([], [], []), ([], [], []), ([], [], [])
    for v in range(nvars):
        real = q_ref[pl.ds(2 * v, NB, stride=rows), :]
        imag = q_ref[pl.ds(2 * v + 1, NB, stride=rows), :]
        weight = weights_ref[v : v + 1, :] * scale
        terms = zip(thirds(real * weight), thirds(imag * weight), thirds(real), thirds(imag))
        for k, (weighted_real, weighted_imag, real, imag) in enumerate(terms):
            left[k].extend((weighted_real, weighted_imag))
            right_real[k].extend((real, imag))
            right_imag[k].extend((imag, -real))
    lhs = jnp.concatenate([jnp.concatenate(term, 1) for term in left], 0)
    rhs = jnp.concatenate([jnp.concatenate(term, 1) for pair in zip(right_real, right_imag) for term in pair], 0)
    product = lax.dot_general(lhs, rhs, (((1,), (1,)), ((), ())), preferred_element_type=F32)
    gram = 0.0
    for i, k in ((1, 1), (0, 2), (2, 0), (0, 1), (1, 0), (0, 0)):
        gram = gram + product[i * NB : (i + 1) * NB, k * LANES : (k + 1) * LANES]
    row, lane = (lax.broadcasted_iota(jnp.int32, (NB, LANES), d) for d in range(2))
    mixed = jnp.where(lane >= row, gram, pltpu.roll(gram, NB, 1))
    half = NB // 2
    packed = jnp.where(lane[:half] < NB, mixed[:half], pltpu.roll(mixed[half:], NB, 1))
    energy = jnp.sum(q_ref[pl.ds(rows - 1, NB, stride=rows), :], axis=0, keepdims=True)
    energy = jnp.where(row[:8] == 0, energy, 0.0)
    for k in range(copies):
        out_ref[k, :half, :] = packed
        out_ref[k, half:, :] = energy


def unpacked(parts_ref):
    total = parts_ref[0]
    for k in range(1, parts_ref.shape[0]):
        total = total + parts_ref[k]
    half = NB // 2
    packed = total[:half]
    row, lane = (lax.broadcasted_iota(jnp.int32, (NB, LANES), d) for d in range(2))
    mixed = jnp.concatenate([packed, pltpu.roll(packed, NB, 1)], 0)
    turned = jnp.transpose(jnp.concatenate([mixed, jnp.zeros_like(mixed)], 0))[:NB]
    real = jnp.where(lane >= row, mixed, turned)
    imag = jnp.where(lane < row, mixed, jnp.where(lane > row, -turned, 0.0))
    return jnp.where(lane < NB, real, pltpu.roll(imag, NB, 1)), jnp.sum(total[half : half + 1], axis=1, keepdims=True)


def shift_top(tops, bottoms, row):
    return [tops[1], tops[2], tops[3], jnp.where(row == 7, bottoms, pltpu.roll(tops[0], 7, 0))]


def shift_bottom(tops, bottoms, row):
    first = jnp.where(row == 0, bottoms[0], pltpu.roll(bottoms[3], 1, 0))
    second = bottoms[0] if tops is None else jnp.where(row == 0, tops, bottoms[0])
    return [first, second, bottoms[1], bottoms[2]]


def one_round(state, offset, ranks, row):
    top, bottom, diag_t, diag_b, beta = state

    def col(rows, i):
        return [r[i] for r in rows]

    total = lambda x: jnp.sum(x, axis=1, keepdims=True)
    tz, bz = col(top, 0), col(bottom, 0)
    uz, wz = shift_top(tz, bz[3], row), shift_top(bz, tz[3], row)
    ux, uix, wx, wix = [], [], [], []
    for i, (u, w) in ((2, (ux, wx)), (3, (uix, wix))):
        t, b = col(top, i), col(bottom, i)
        u += shift_bottom(t[0], b, row)
        w += shift_bottom(b[0], t, row)
    inner = []
    for v in range(GROUPS):
        inner.append([(total(z * x), total(z * ix)) for z in (uz[v], wz[v]) for x, ix in ((ux[v], uix[v]), (wx[v], wix[v]))])
    cos, off, img, new_dt, new_db = [], [], [], [], []
    wide = lambda x: jnp.broadcast_to(x, (8, LANES))
    new_top, new_bottom = [], []
    for v in range(GROUPS):
        real, imag = beta[v]
        at, ab = diag_t[v], diag_b[v]
        sign = jnp.where(ranks[v] > offset, 1.0, -1.0)
        delta = sign * (ab - at)
        four = real * real + imag * imag
        square = delta * delta + four
        high = square * lax.rsqrt(jnp.maximum(square, 1e-37)) + DAMPING * (ab + at)
        upper = high + delta
        inverse = lax.rsqrt(upper * upper + four)
        signed = sign * inverse
        c, r, i = upper * inverse, signed * real, signed * imag
        moved = (four * inverse) * (signed * high)
        new_dt.append(at - moved)
        new_db.append(ab + moved)
        cos.append(c); off.append(r); img.append(i)
        (zt, izt, xt, ixt), (zb, izb, xb, ixb) = top[v], bottom[v]
        new_top.append((c * zt - r * zb - i * izb, c * izt - r * izb + i * zb, c * xt - r * xb - i * ixb, c * ixt - r * ixb + i * xb))
        new_bottom.append((c * zb + r * zt - i * izt, c * izb + r * izt + i * zt, c * xb + r * xt - i * ixt, c * ixb + r * ixt + i * xt))
    c1, r1, i1 = shift_top(cos, cos[3], row), shift_top(off, -off[3], row), shift_top(img, img[3], row)
    c2, r2, i2 = shift_bottom(None, cos, row), shift_bottom(-off[0], off, row), shift_bottom(None, img, row)
    new_beta = []
    for v in range(GROUPS):
        uu, uw, wu, ww = inner[v]
        ca, ra, ia, cb, rb, ib = c1[v], r1[v], i1[v], c2[v], r2[v], i2[v]
        ur = cb * uu[0] + rb * uw[0] - ib * uw[1]
        ui = cb * uu[1] + rb * uw[1] + ib * uw[0]
        wr = cb * wu[0] + rb * ww[0] - ib * ww[1]
        wi = cb * wu[1] + rb * ww[1] + ib * ww[0]
        new_beta.append((wide(ca * ur - ra * wr + ia * wi), wide(ca * ui - ra * wi - ia * wr)))
    tops = [shift_top(col(new_top, i), new_bottom[3][i], row) for i in range(4)]
    bottoms = [shift_bottom(new_top[0][i], col(new_bottom, i), row) for i in range(4)]
    return (list(zip(*tops)), list(zip(*bottoms)), shift_top(new_dt, new_db[3], row),
            shift_bottom(new_dt[0], new_db, row), new_beta)


def split(x):
    high = x.astype(jnp.bfloat16)
    return high, (x - high.astype(F32)).astype(jnp.bfloat16)


def modes_kernel(parts_ref, q_ref, modes_ref, spectrum_ref, gram_ref, rows_ref):
    lane = lax.broadcasted_iota(jnp.int32, (8, LANES), 1)
    sub = lax.broadcasted_iota(jnp.int32, (8, LANES), 0)
    gram_ref[...], energy = unpacked(parts_ref)
    for v in range(GROUPS):
        for s in range(8):
            p = GROUPS * s + v
            rows_ref[8 * v + s : 8 * v + s + 1, :] = gram_ref[p : p + 1, :]
            rows_ref[32 + 8 * v + s : 33 + 8 * v + s, :] = gram_ref[63 - p : 64 - p, :]
    flip = jnp.where(lane < NB, -1.0, 1.0)
    top, bottom, diag_t, diag_b, ranks = [], [], [], [], []
    for v in range(GROUPS):
        p = GROUPS * sub + v
        for base, index, rows, diag in ((0, p, top, diag_t), (32, 63 - p, bottom, diag_b)):
            z = rows_ref[base + 8 * v : base + 8 * v + 8, :]
            x = jnp.where(lane == index, 1.0, 0.0)
            ix = jnp.where(lane == index + NB, 1.0, 0.0)
            rows.append((z + z, (flip + flip) * pltpu.roll(z, NB, 1), x, ix))
            diag.append(jnp.broadcast_to(jnp.sum(z * x, axis=1, keepdims=True), (8, LANES)))
        ranks.append(jnp.where(p == 0, 1000, p))
    def inner(z, x):
        return jnp.broadcast_to(jnp.sum(z * x, axis=1, keepdims=True), (8, LANES))

    beta = [(inner(t[0], b[2]), inner(t[0], b[3])) for t, b in zip(top, bottom)]
    flat, tree = jax.tree.flatten((top, bottom, diag_t, diag_b, beta))

    def some_rounds(step, flat):
        state = jax.tree.unflatten(tree, flat)
        for i in range(UNROLL):
            offset = 31 - jnp.abs(lax.rem(step * UNROLL + i, NB - 1) - 31)
            state = one_round(state, offset, ranks, sub)
        return jax.tree.flatten(state)[0]

    rounds = SWEEPS * (NB - 1)
    flat = lax.fori_loop(0, rounds // UNROLL, some_rounds, flat)
    state = jax.tree.unflatten(tree, flat)
    for i in range(rounds // UNROLL * UNROLL, rounds):
        state = one_round(state, 31 - abs(i % (NB - 1) - 31), ranks, sub)
    top, bottom, diag_t, diag_b, _ = state
    eigen = jnp.zeros((8, LANES), F32)
    left = lane < NB
    for v in range(GROUPS):
        for rows, diag, low in ((top[v], diag_t[v], True), (bottom[v], diag_b[v], False)):
            x, ix = rows[2], rows[3]
            sum_real = jnp.sum(jnp.where(left, x, 0.0), axis=1, keepdims=True)
            sum_imag = -jnp.sum(jnp.where(left, 0.0, x), axis=1, keepdims=True)
            magnitude = jnp.sqrt(sum_real * sum_real + sum_imag * sum_imag)
            scaling = 1.0 / (jnp.maximum(magnitude, 1.0) * jnp.sqrt(NB * (diag + 1e-06)))
            phase_r, phase_i = sum_real * scaling, -sum_imag * scaling
            coef = jnp.where(left, 1.0, -1.0) * (x * phase_r - ix * phase_i)
            index = GROUPS * sub + v if low else 63 - GROUPS * sub - v
            eigen = eigen + jnp.where(lane == index, diag, 0.0)
            for s in range(8):
                p = GROUPS * s + v
                row = p if low else 63 - p
                rows_ref[row : row + 1, :] = coef[s : s + 1, :]
    spectrum = jnp.sum(eigen, axis=0, keepdims=True) * (NB * NB) / energy
    spectrum_ref[...] = spectrum[:, :NB]
    rows = q_ref.shape[0] // NB
    nparts = rows - 1
    coefs = rows_ref[...]
    high, low = split(jnp.concatenate([coefs[:, :NB], coefs[:, NB:]], 0))
    lhs = jnp.concatenate([high, high, low], 1)
    for v in range(nparts // 2):
        real = q_ref[pl.ds(2 * v, NB, stride=rows), :]
        imag = q_ref[pl.ds(2 * v + 1, NB, stride=rows), :]
        high, low = split(jnp.concatenate([real, imag], 1))
        out = jnp.dot(lhs, jnp.concatenate([high, low, high], 0), preferred_element_type=F32)
        modes_ref[pl.ds(2 * v, NB, stride=nparts), :] = out[:NB, :LANES] - out[NB:, LANES:]
        modes_ref[pl.ds(2 * v + 1, NB, stride=nparts), :] = out[:NB, LANES:] + out[NB:, :LANES]


def spec(space):
    return pl.BlockSpec(memory_space=space)


def half_spectra(tail, offsets, freqs, own):
    nvars, nfft, npts = own.shape
    return pl.pallas_call(
        functools.partial(half_spectra_kernel, tail, nvars),
        out_shape=jax.ShapeDtypeStruct((NB * 2 * nvars, npts), F32),
        in_specs=[spec(pl.ANY)] * 3,
        scratch_shapes=[
            pltpu.SMEM(offsets.shape, jnp.int32),
            pltpu.VMEM(freqs.shape, jnp.int32),
            pltpu.VMEM((nvars, nfft, npts), F32),
            pltpu.SemaphoreType.DMA((nvars + 2,)),
        ],
        compiler_params=pltpu.CompilerParams(vmem_limit_bytes=(60 if tail else 16) << 20),
        cost_estimate=pl.CostEstimate(flops=12 * NB * 2 * nfft * nvars * npts, bytes_accessed=4 * own.size, transcendentals=0),
        name="tail" if tail else "head",
    )(offsets, freqs, own)


def body(snapshots, weights, offsets, freqs):
    nfft, nvars, npts = snapshots.shape
    nfreq = freqs.shape[0]
    nblocks = lax.axis_size("blk")
    nparts = lax.axis_size("pts")
    rows = 2 * nvars + 1
    own = jnp.transpose(snapshots, (1, 0, 2))
    freqs = freqs.reshape(1, nfreq)
    offsets = offsets.reshape(1, nblocks)
    tail = half_spectra(True, offsets, freqs, own)
    tail = lax.ppermute(tail, "blk", [(i + 1, i) for i in range(nblocks - 1)])
    head = half_spectra(False, offsets, freqs, own)
    scale = 1.0 / (nblocks * nvars * npts * nparts)
    spectra = pl.pallas_call(
        functools.partial(join_kernel, scale),
        out_shape=jax.ShapeDtypeStruct((nfreq * rows, npts), F32),
        compiler_params=PARAMS,
        name="join",
    )(head, tail, weights)
    grouped = lax.all_to_all(
        spectra.reshape(nfreq, 1, rows, 1, npts), "blk", split_axis=0, concat_axis=1, tiled=True
    ).reshape(nblocks * rows, npts)
    gram = pl.pallas_call(
        functools.partial(gram_kernel, scale, nparts),
        out_shape=jax.ShapeDtypeStruct((nparts, nblocks // 2 + 8, LANES), F32),
        compiler_params=PARAMS,
        name="gram",
    )(grouped, weights)
    parts = lax.all_to_all(gram, "pts", split_axis=0, concat_axis=0, tiled=True)
    modes, spectrum = pl.pallas_call(
        modes_kernel,
        out_shape=[
            jax.ShapeDtypeStruct((nblocks * 2 * nvars, npts), F32),
            jax.ShapeDtypeStruct((1, nblocks), F32),
        ],
        scratch_shapes=[pltpu.VMEM((nblocks, LANES), F32)] * 2,
        compiler_params=PARAMS,
        name="modes",
    )(parts, grouped)
    modes = modes.reshape(1, nblocks, nvars, 2, npts).transpose(0, 1, 3, 2, 4)
    return modes, spectrum


def solution(mesh):
    return jax.shard_map(
        body,
        mesh=mesh,
        in_specs=(P("blk", None, "pts"), P(None, "pts"), P(), P()),
        out_specs=(P("blk", None, None, None, "pts"), P("blk", None)),
        check_vma=False,
    )
```

```python
import functools
import math

import jax
import jax.numpy as jnp
from jax import lax
from jax.experimental import pallas as pl
from jax.experimental.pallas import tpu as pltpu
from jax.sharding import PartitionSpec as P

SWEEPS = 2
HIGH = lax.Precision.HIGHEST
DAMPING = 0.01
F32 = jnp.float32
NFFT = 256
NB = 64
LANES = 128
GROUPS = 4
UNROLL = 20
PARAMS = pltpu.CompilerParams(vmem_limit_bytes=16 << 20)


def half_spectra_kernel(tail, nvars, offsets_hbm, freqs_hbm, own_ref, out_ref, offsets_ref, freqs_ref, data_ref, sem):
    small = [
        pltpu.make_async_copy(offsets_hbm, offsets_ref, sem.at[nvars]),
        pltpu.make_async_copy(freqs_hbm, freqs_ref, sem.at[nvars + 1]),
    ]
    copies = [pltpu.make_async_copy(own_ref.at[v], data_ref.at[v], sem.at[v]) for v in range(nvars)]
    for copy in small + copies:
        copy.start()
    block = lax.axis_index("blk")
    if tail:
        block = jnp.where(block == 0, NB, block) - 1
    for copy in small:
        copy.wait()
    offset = offsets_ref[0, block]
    snapshot = lax.broadcasted_iota(jnp.int32, (1, NFFT), 1)
    lag = jnp.bitwise_and(snapshot - offset, NFFT - 1)
    valid = snapshot < offset if tail else snapshot >= offset
    unit = 2.0 * math.pi / NFFT
    hann = jnp.where(valid, 0.5 - 0.5 * jnp.cos(unit * lag.astype(F32)), 0.0) / math.sqrt(NFFT)
    square = (NB, NB)
    same = lax.broadcasted_iota(jnp.int32, square, 0) == lax.broadcasted_iota(jnp.int32, square, 1)
    freqs = jnp.sum(jnp.where(same, freqs_ref[...].astype(F32), 0.0), axis=1, keepdims=True).astype(jnp.int32)
    angle = unit * jnp.bitwise_and(freqs * lag, NFFT - 1).astype(F32)
    table = jnp.concatenate([hann * jnp.cos(angle), -hann * jnp.sin(angle)], 0)
    for copy in copies:
        copy.wait()
    data = jnp.concatenate([data_ref[v] for v in range(nvars)], 1)
    result = jnp.dot(table, data, precision=HIGH, preferred_element_type=F32)
    for v in range(nvars):
        for part in range(2):
            piece = result[part * NB : (part + 1) * NB, v * LANES : (v + 1) * LANES]
            out_ref[pl.ds(2 * v + part, NB, stride=2 * nvars), :] = piece


def join_kernel(scale, head_ref, tail_ref, weights_ref, out_ref):
    nvars = weights_ref.shape[0]
    rows = 2 * nvars + 1
    energy = jnp.zeros((1, LANES), F32)
    for j in range(2 * nvars):
        value = head_ref[pl.ds(j, NB, stride=2 * nvars), :] + tail_ref[pl.ds(j, NB, stride=2 * nvars), :]
        out_ref[pl.ds(j, NB, stride=rows), :] = value
        weight = weights_ref[j // 2 : j // 2 + 1, :] * scale
        energy = energy + jnp.sum(value * value, axis=0, keepdims=True) * weight
    out_ref[pl.ds(rows - 1, NB, stride=rows), :] = jnp.broadcast_to(energy, (NB, LANES))


def thirds(x):
    high = x.astype(jnp.bfloat16)
    rest = x - high.astype(F32)
    middle = rest.astype(jnp.bfloat16)
    return high, middle, (rest - middle.astype(F32)).astype(jnp.bfloat16)


def gram_kernel(scale, copies, q_ref, weights_ref, out_ref):
    nvars = weights_ref.shape[0]
    rows = 2 * nvars + 1
    left, right_real, right_imag = ([], [], []), ([], [], []), ([], [], [])
    for v in range(nvars):
        real = q_ref[pl.ds(2 * v, NB, stride=rows), :]
        imag = q_ref[pl.ds(2 * v + 1, NB, stride=rows), :]
        weight = weights_ref[v : v + 1, :] * scale
        terms = zip(thirds(real * weight), thirds(imag * weight), thirds(real), thirds(imag))
        for k, (weighted_real, weighted_imag, real, imag) in enumerate(terms):
            left[k].extend((weighted_real, weighted_imag))
            right_real[k].extend((real, imag))
            right_imag[k].extend((imag, -real))
    lhs = jnp.concatenate([jnp.concatenate(term, 1) for term in left], 0)
    rhs = jnp.concatenate([jnp.concatenate(term, 1) for pair in zip(right_real, right_imag) for term in pair], 0)
    product = lax.dot_general(lhs, rhs, (((1,), (1,)), ((), ())), preferred_element_type=F32)
    gram = 0.0
    for i, k in ((1, 1), (0, 2), (2, 0), (0, 1), (1, 0), (0, 0)):
        gram = gram + product[i * NB : (i + 1) * NB, k * LANES : (k + 1) * LANES]
    row, lane = (lax.broadcasted_iota(jnp.int32, (NB, LANES), d) for d in range(2))
    mixed = jnp.where(lane >= row, gram, pltpu.roll(gram, NB, 1))
    half = NB // 2
    packed = jnp.where(lane[:half] < NB, mixed[:half], pltpu.roll(mixed[half:], NB, 1))
    energy = jnp.sum(q_ref[pl.ds(rows - 1, NB, stride=rows), :], axis=0, keepdims=True)
    energy = jnp.where(row[:8] == 0, energy, 0.0)
    for k in range(copies):
        out_ref[k, :half, :] = packed
        out_ref[k, half:, :] = energy


def unpacked(parts_ref):
    total = parts_ref[0]
    for k in range(1, parts_ref.shape[0]):
        total = total + parts_ref[k]
    half = NB // 2
    packed = total[:half]
    row, lane = (lax.broadcasted_iota(jnp.int32, (NB, LANES), d) for d in range(2))
    mixed = jnp.concatenate([packed, pltpu.roll(packed, NB, 1)], 0)
    turned = jnp.transpose(jnp.concatenate([mixed, jnp.zeros_like(mixed)], 0))[:NB]
    real = jnp.where(lane >= row, mixed, turned)
    imag = jnp.where(lane < row, mixed, jnp.where(lane > row, -turned, 0.0))
    return jnp.where(lane < NB, real, pltpu.roll(imag, NB, 1)), jnp.sum(total[half : half + 1], axis=1, keepdims=True)


def shift_top(tops, bottoms, row):
    return [tops[1], tops[2], tops[3], jnp.where(row == 7, bottoms, pltpu.roll(tops[0], 7, 0))]


def shift_bottom(tops, bottoms, row):
    first = jnp.where(row == 0, bottoms[0], pltpu.roll(bottoms[3], 1, 0))
    second = bottoms[0] if tops is None else jnp.where(row == 0, tops, bottoms[0])
    return [first, second, bottoms[1], bottoms[2]]


def one_round(state, offset, ranks, row):
    top, bottom, diag_t, diag_b, beta = state

    def col(rows, i):
        return [r[i] for r in rows]

    total = lambda x: jnp.sum(x, axis=1, keepdims=True)
    tz, bz = col(top, 0), col(bottom, 0)
    uz, wz = shift_top(tz, bz[3], row), shift_top(bz, tz[3], row)
    ux, uix, wx, wix = [], [], [], []
    for i, (u, w) in ((2, (ux, wx)), (3, (uix, wix))):
        t, b = col(top, i), col(bottom, i)
        u += shift_bottom(t[0], b, row)
        w += shift_bottom(b[0], t, row)
    inner = []
    for v in range(GROUPS):
        inner.append([(total(z * x), total(z * ix)) for z in (uz[v], wz[v]) for x, ix in ((ux[v], uix[v]), (wx[v], wix[v]))])
    cos, off, img, new_dt, new_db = [], [], [], [], []
    wide = lambda x: jnp.broadcast_to(x, (8, LANES))
    new_top, new_bottom = [], []
    for v in range(GROUPS):
        real, imag = beta[v]
        at, ab = diag_t[v], diag_b[v]
        sign = jnp.where(ranks[v] > offset, 1.0, -1.0)
        delta = sign * (ab - at)
        four = real * real + imag * imag
        square = delta * delta + four
        high = square * lax.rsqrt(jnp.maximum(square, 1e-37)) + DAMPING * (ab + at)
        upper = high + delta
        inverse = lax.rsqrt(upper * upper + four)
        signed = sign * inverse
        c, r, i = upper * inverse, signed * real, signed * imag
        moved = (four * inverse) * (signed * high)
        new_dt.append(at - moved)
        new_db.append(ab + moved)
        cos.append(c); off.append(r); img.append(i)
        (zt, izt, xt, ixt), (zb, izb, xb, ixb) = top[v], bottom[v]
        new_top.append((c * zt - r * zb - i * izb, c * izt - r * izb + i * zb, c * xt - r * xb - i * ixb, c * ixt - r * ixb + i * xb))
        new_bottom.append((c * zb + r * zt - i * izt, c * izb + r * izt + i * zt, c * xb + r * xt - i * ixt, c * ixb + r * ixt + i * xt))
    c1, r1, i1 = shift_top(cos, cos[3], row), shift_top(off, -off[3], row), shift_top(img, img[3], row)
    c2, r2, i2 = shift_bottom(None, cos, row), shift_bottom(-off[0], off, row), shift_bottom(None, img, row)
    new_beta = []
    for v in range(GROUPS):
        uu, uw, wu, ww = inner[v]
        ca, ra, ia, cb, rb, ib = c1[v], r1[v], i1[v], c2[v], r2[v], i2[v]
        ur = cb * uu[0] + rb * uw[0] - ib * uw[1]
        ui = cb * uu[1] + rb * uw[1] + ib * uw[0]
        wr = cb * wu[0] + rb * ww[0] - ib * ww[1]
        wi = cb * wu[1] + rb * ww[1] + ib * ww[0]
        new_beta.append((wide(ca * ur - ra * wr + ia * wi), wide(ca * ui - ra * wi - ia * wr)))
    tops = [shift_top(col(new_top, i), new_bottom[3][i], row) for i in range(4)]
    bottoms = [shift_bottom(new_top[0][i], col(new_bottom, i), row) for i in range(4)]
    return (list(zip(*tops)), list(zip(*bottoms)), shift_top(new_dt, new_db[3], row),
            shift_bottom(new_dt[0], new_db, row), new_beta)


def split(x):
    high = x.astype(jnp.bfloat16)
    return high, (x - high.astype(F32)).astype(jnp.bfloat16)


def modes_kernel(parts_ref, q_ref, modes_ref, spectrum_ref, gram_ref, rows_ref):
    lane = lax.broadcasted_iota(jnp.int32, (8, LANES), 1)
    sub = lax.broadcasted_iota(jnp.int32, (8, LANES), 0)
    gram_ref[...], energy = unpacked(parts_ref)
    for v in range(GROUPS):
        for s in range(8):
            p = GROUPS * s + v
            rows_ref[8 * v + s : 8 * v + s + 1, :] = gram_ref[p : p + 1, :]
            rows_ref[32 + 8 * v + s : 33 + 8 * v + s, :] = gram_ref[63 - p : 64 - p, :]
    flip = jnp.where(lane < NB, -1.0, 1.0)
    top, bottom, diag_t, diag_b, ranks = [], [], [], [], []
    for v in range(GROUPS):
        p = GROUPS * sub + v
        for base, index, rows, diag in ((0, p, top, diag_t), (32, 63 - p, bottom, diag_b)):
            z = rows_ref[base + 8 * v : base + 8 * v + 8, :]
            x = jnp.where(lane == index, 1.0, 0.0)
            ix = jnp.where(lane == index + NB, 1.0, 0.0)
            rows.append((z + z, (flip + flip) * pltpu.roll(z, NB, 1), x, ix))
            diag.append(jnp.broadcast_to(jnp.sum(z * x, axis=1, keepdims=True), (8, LANES)))
        ranks.append(jnp.where(p == 0, 1000, p))
    def inner(z, x):
        return jnp.broadcast_to(jnp.sum(z * x, axis=1, keepdims=True), (8, LANES))

    beta = [(inner(t[0], b[2]), inner(t[0], b[3])) for t, b in zip(top, bottom)]
    flat, tree = jax.tree.flatten((top, bottom, diag_t, diag_b, beta))

    def some_rounds(step, flat):
        state = jax.tree.unflatten(tree, flat)
        for i in range(UNROLL):
            offset = 31 - jnp.abs(lax.rem(step * UNROLL + i, NB - 1) - 31)
            state = one_round(state, offset, ranks, sub)
        return jax.tree.flatten(state)[0]

    rounds = SWEEPS * (NB - 1)
    flat = lax.fori_loop(0, rounds // UNROLL, some_rounds, flat)
    state = jax.tree.unflatten(tree, flat)
    for i in range(rounds // UNROLL * UNROLL, rounds):
        state = one_round(state, 31 - abs(i % (NB - 1) - 31), ranks, sub)
    top, bottom, diag_t, diag_b, _ = state
    eigen = jnp.zeros((8, LANES), F32)
    left = lane < NB
    for v in range(GROUPS):
        for rows, diag, low in ((top[v], diag_t[v], True), (bottom[v], diag_b[v], False)):
            x, ix = rows[2], rows[3]
            sum_real = jnp.sum(jnp.where(left, x, 0.0), axis=1, keepdims=True)
            sum_imag = -jnp.sum(jnp.where(left, 0.0, x), axis=1, keepdims=True)
            magnitude = jnp.sqrt(sum_real * sum_real + sum_imag * sum_imag)
            scaling = 1.0 / (jnp.maximum(magnitude, 1.0) * jnp.sqrt(NB * (diag + 1e-06)))
            phase_r, phase_i = sum_real * scaling, -sum_imag * scaling
            coef = jnp.where(left, 1.0, -1.0) * (x * phase_r - ix * phase_i)
            index = GROUPS * sub + v if low else 63 - GROUPS * sub - v
            eigen = eigen + jnp.where(lane == index, diag, 0.0)
            for s in range(8):
                p = GROUPS * s + v
                row = p if low else 63 - p
                rows_ref[row : row + 1, :] = coef[s : s + 1, :]
    spectrum = jnp.sum(eigen, axis=0, keepdims=True) * (NB * NB) / energy
    spectrum_ref[...] = spectrum[:, :NB]
    rows = q_ref.shape[0] // NB
    nparts = rows - 1
    coefs = rows_ref[...]
    high, low = split(jnp.concatenate([coefs[:, :NB], coefs[:, NB:]], 0))
    lhs = jnp.concatenate([high, high, low], 1)
    for v in range(nparts // 2):
        real = q_ref[pl.ds(2 * v, NB, stride=rows), :]
        imag = q_ref[pl.ds(2 * v + 1, NB, stride=rows), :]
        high, low = split(jnp.concatenate([real, imag], 1))
        out = jnp.dot(lhs, jnp.concatenate([high, low, high], 0), preferred_element_type=F32)
        modes_ref[pl.ds(2 * v, NB, stride=nparts), :] = out[:NB, :LANES] - out[NB:, LANES:]
        modes_ref[pl.ds(2 * v + 1, NB, stride=nparts), :] = out[:NB, LANES:] + out[NB:, :LANES]


def spec(space):
    return pl.BlockSpec(memory_space=space)


def half_spectra(tail, offsets, freqs, own):
    nvars, nfft, npts = own.shape
    return pl.pallas_call(
        functools.partial(half_spectra_kernel, tail, nvars),
        out_shape=jax.ShapeDtypeStruct((NB * 2 * nvars, npts), F32),
        in_specs=[spec(pl.ANY)] * 3,
        scratch_shapes=[
            pltpu.SMEM(offsets.shape, jnp.int32),
            pltpu.VMEM(freqs.shape, jnp.int32),
            pltpu.VMEM((nvars, nfft, npts), F32),
            pltpu.SemaphoreType.DMA((nvars + 2,)),
        ],
        compiler_params=pltpu.CompilerParams(vmem_limit_bytes=16 << 20),
        cost_estimate=pl.CostEstimate(flops=12 * NB * 2 * nfft * nvars * npts, bytes_accessed=4 * own.size, transcendentals=0),
        name="tail" if tail else "head",
    )(offsets, freqs, own)


def body(snapshots, weights, offsets, freqs):
    nfft, nvars, npts = snapshots.shape
    nfreq = freqs.shape[0]
    nblocks = lax.axis_size("blk")
    nparts = lax.axis_size("pts")
    rows = 2 * nvars + 1
    own = jnp.transpose(snapshots, (1, 0, 2))
    freqs = freqs.reshape(1, nfreq)
    offsets = offsets.reshape(1, nblocks)
    tail = half_spectra(True, *(pltpu.with_memory_space_constraint(x, pltpu.HBM) for x in (offsets, freqs, own)))
    tail = lax.ppermute(tail, "blk", [(i + 1, i) for i in range(nblocks - 1)])
    head = half_spectra(False, offsets, freqs, own)
    scale = 1.0 / (nblocks * nvars * npts * nparts)
    spectra = pl.pallas_call(
        functools.partial(join_kernel, scale),
        out_shape=jax.ShapeDtypeStruct((nfreq * rows, npts), F32),
        compiler_params=PARAMS,
        name="join",
    )(head, tail, weights)
    grouped = lax.all_to_all(
        spectra.reshape(nfreq, 1, rows, 1, npts), "blk", split_axis=0, concat_axis=1, tiled=True
    ).reshape(nblocks * rows, npts)
    gram = pl.pallas_call(
        functools.partial(gram_kernel, scale, nparts),
        out_shape=jax.ShapeDtypeStruct((nparts, nblocks // 2 + 8, LANES), F32),
        compiler_params=PARAMS,
        name="gram",
    )(grouped, weights)
    parts = lax.all_to_all(gram, "pts", split_axis=0, concat_axis=0, tiled=True)
    modes, spectrum = pl.pallas_call(
        modes_kernel,
        out_shape=[
            jax.ShapeDtypeStruct((nblocks * 2 * nvars, npts), F32),
            jax.ShapeDtypeStruct((1, nblocks), F32),
        ],
        scratch_shapes=[pltpu.VMEM((nblocks, LANES), F32)] * 2,
        compiler_params=PARAMS,
        name="modes",
    )(parts, grouped)
    modes = modes.reshape(1, nblocks, nvars, 2, npts).transpose(0, 1, 3, 2, 4)
    return modes, spectrum


def solution(mesh):
    return jax.shard_map(
        body,
        mesh=mesh,
        in_specs=(P("blk", None, "pts"), P(None, "pts"), P(), P()),
        out_specs=(P("blk", None, None, None, "pts"), P("blk", None)),
        check_vma=False,
    )
```
